32 devices in a mesh: groups: 2 (over x), ctx: 16 (over z, y, core).
Axes of the slice: x: 2, y: 2, z: 4, core: 2. Of those that a mesh axis runs over, the one named last changes fastest.
Arguments:
- queries: bfloat16 [2560, 4096], P(('groups', 'ctx')), parts along dimension 0, may hold values from -200 to 200
- fresh_key_value: bfloat16 [2, 2560, 512], P(None, ('groups', 'ctx')), parts along dimension 1, may hold values from -6 to 6
- cache_key_value: bfloat16 [2, 4096, 512], P(None, ('groups', 'ctx')), parts along dimension 1, may hold values from -6 to 6
- residual: bfloat16 [2560, 2048], P(('groups', 'ctx')), parts along dimension 0, may hold values from -6 to 6
- norm_gain: float32 [2048], replicated, may hold values from 0.5 to 2
- out_proj: bfloat16 [4096, 2048], P('ctx'), may hold values from -0.09375 to 0.09375
- w_gate_up: bfloat16 [32, 2048, 1536], P('ctx'), may hold values from -0.125 to 0.125
- w_down: bfloat16 [32, 768, 2048], P('ctx'), may hold values from -0.21875 to 0.21875
- route_ids: int32 [2560, 8], P(('groups', 'ctx')), parts along dimension 0, may hold values from 0 to 31, all different within a row; in each aligned block of 80 rows (0 to 79, 80 to 159, ...) at most 30 rows name the same one
- route_weights: float32 [2560, 8], P(('groups', 'ctx')), parts along dimension 0, may hold values from 0.05 to 1
- placement: int32 [32], replicated, may hold values from 0 to 31, each once
Outputs:
- hidden: bfloat16 [2560, 2048], P(('groups', 'ctx')), parts along dimension 0
- expert_out: bfloat16 [2560, 2048], P(('groups', 'ctx')), parts along dimension 0
The draws below stay inside these ranges and needn't reach their ends.
There are 2 independent parts, one for each index of `groups`. The reference program is written for one: setup_inputs(seed, part) draws one part's arguments, and reference() takes and returns one part's arrays. A program takes and returns all parts, laid end to end along the dimension named above; an argument that names none is the same for every part. Nothing has to cross between parts.
Inputs may be any that keep to these rules, and one draw needn't show every extreme that they name: `route_ids`: among the rows of one index of ctx, no expert is named by more than 30 rows, a bound that some block reaches. `placement`: every slot once; slot s is the first index of w_gate_up and w_down.
All inputs are finite; a program needn't handle non-finite values.
Results may differ from the reference program's by a relative error of at most 0.017.
Values may be sent and summed in bfloat16 or wider, within the bound.
A program may use at most 128 MiB of HBM per device.

```python
import math
import jax
import jax.numpy as jnp
import numpy as np
from jax import lax

D = 2048
QUERY_HEADS = 32
KEY_VALUE_HEADS = 4
HEAD_SIZE = 128
FF = 768
TOPK = 8
ROWS_DEV = 80
EXPERTS = 32
WINDOW_ROWS = 1280
CACHED_KEYS = 2048
MOST = 30
N_CTX = 16


def attention_pair(key):
    query_key = jax.random.fold_in(key, 101)
    stored_key = jax.random.fold_in(key, 102)
    random_value_key = jax.random.fold_in(key, 103)
    queries = 2.5 * jax.random.truncated_normal(query_key, -6.0, 6.0, (WINDOW_ROWS, QUERY_HEADS * HEAD_SIZE), jnp.float32)
    stored_keys = jax.random.truncated_normal(stored_key, -6.0, 6.0, (CACHED_KEYS, KEY_VALUE_HEADS * HEAD_SIZE), jnp.float32)
    stored_values = jax.random.truncated_normal(random_value_key, -6.0, 6.0, (CACHED_KEYS, KEY_VALUE_HEADS * HEAD_SIZE), jnp.float32)
    return (queries, stored_keys, stored_values)


def draw_queries(key, part):
    queries, stored_keys, stored_values = attention_pair(key)
    return queries.astype(jnp.bfloat16)


def draw_cache_key_value(key, part):
    queries, stored_keys, stored_values = attention_pair(key)
    return jnp.stack([stored_keys, stored_values], axis=0).astype(jnp.bfloat16)


def level_of(rng, dims, cuts, low, high):
    level = 1.0
    for dim, blocks in cuts:
        steps = jax.random.uniform(jax.random.fold_in(jax.random.fold_in(rng, 6), dim), (blocks,), jnp.float32, low / len(cuts), high / len(cuts))
        level = level * jnp.repeat(jnp.exp(steps), dims[dim] // blocks).reshape((-1,) + (1,) * (len(dims) - 1 - dim))
    return level


def routed_block(own_key, own, number, rows, number_of, top, reach, slope):
    ranking = jax.random.permutation(own_key, number_of)
    heavy_load, common = shares(number_of, rows * top, reach, slope, True), shares(number_of, rows * top, reach, slope, False)
    places = jnp.arange(number_of)

    def named(sizes, turn):
        used = int((sizes > 0).sum())
        fixed = max(1, used // 4)
        shifted = fixed + (places - fixed + turn * (used - fixed)) % max(1, number_of - fixed)
        return jnp.zeros((number_of,), jnp.int32).at[ranking[jnp.where(places < fixed, places, shifted)]].set(jnp.asarray(sizes, jnp.int32))

    sizes = jnp.where(number % 4 == 0, named(heavy_load, number // 4), named(common, number - number // 4 - 1))
    mixed = jax.random.permutation(jax.random.fold_in(own, 3), number_of)
    giver, taker = mixed[0:number_of // 2 * 2:2], mixed[1:number_of // 2 * 2:2]
    margin = jnp.minimum(sizes[giver] - 1, reach - sizes[taker]) // 2
    margin = jnp.where((giver == ranking[0]) | (taker == ranking[0]) | (sizes[taker] == 0), 0, jnp.maximum(margin, 0))
    shifted = jax.random.randint(jax.random.fold_in(own, 4), (number_of // 2,), 0, 1 << 20) % (margin + 1)
    sizes = sizes.at[giver].add(-shifted).at[taker].add(shifted)
    labels = jnp.searchsorted(jnp.cumsum(sizes), jnp.arange(rows * top), side="right").astype(jnp.int32)
    listing = labels.reshape(top, rows).T
    listing = listing[jax.random.permutation(jax.random.fold_in(own, 1), rows)]
    turn = jax.random.randint(jax.random.fold_in(own, 2), (rows, 1), 0, top)
    return jnp.take_along_axis(listing, (jnp.arange(top)[None, :] + turn) % top, axis=1)


def shares(number_of, total, bound, lean, full):
    weights = [(1 << 20) // math.isqrt(rank ** lean) + 1 for rank in range(1, number_of + 1)]
    largest = bound if full else min(bound, max(-(-total // number_of), total * weights[0] // sum(weights)))
    least = 1 if total - largest >= number_of - 1 else 0
    holding, surplus = [largest] + [least] * (number_of - 1), total - largest - least * (number_of - 1)
    while surplus > 0:
        candidates = [i for i in range(1, number_of) if holding[i] < largest] or [i for i in range(1, number_of) if holding[i] < bound]
        whole, remaining = sum([weights[i] for i in candidates]), surplus
        for i in candidates:
            addition = min(bound - holding[i], max(1, remaining * weights[i] // whole), surplus)
            holding[i] = holding[i] + addition
            surplus = surplus - addition
    return np.array(holding)


def centred(own_key, extent, spread, most, cuts=(), kind=jnp.bfloat16):
    values = jax.random.normal(own_key, extent, jnp.float32) * spread
    if len(cuts) > 0:
        values = level_of(own_key, extent, cuts, -0.22, 0.18) * values
    return jnp.clip(values, min=-most, max=most).astype(kind)


def setup_inputs(seed: int = 0, part: int = 0) -> dict:
    key_list = jax.random.split(jax.random.key(seed), 12)
    part_keys = jax.random.split(jax.random.fold_in(key_list[11], part), 12)
    queries = draw_queries(jax.random.fold_in(jax.random.fold_in(key_list[11], part), 71), part)
    fresh_key_value = centred(part_keys[1], (2, WINDOW_ROWS, KEY_VALUE_HEADS * HEAD_SIZE), 1.0, 6.0, ((1, 16),))
    cache_key_value = draw_cache_key_value(jax.random.fold_in(jax.random.fold_in(key_list[11], part), 71), part)
    residual = centred(part_keys[3], (WINDOW_ROWS, D), 1.0, 6.0, ((0, 16),))
    norm_gain = jnp.clip(jnp.exp(jax.random.uniform(key_list[4], (D,), jnp.float32, math.log(0.5), math.log(2.0))), 0.5, 2.0)
    out_proj = centred(key_list[5], (QUERY_HEADS * HEAD_SIZE, D), (QUERY_HEADS * HEAD_SIZE) ** -0.5, 0.09375, ((0, 16),))
    w_gate_up = centred(key_list[6], (EXPERTS, D, 2 * FF), D ** -0.5, 0.125, ((0, 16),))
    w_down = centred(key_list[7], (EXPERTS, FF, D), FF ** -0.5, 0.21875, ((0, 16),))
    route_ids_keys = jax.random.split(jax.random.fold_in(part_keys[8], 1), WINDOW_ROWS // ROWS_DEV)
    route_ids_turns = jax.random.permutation(jax.random.fold_in(part_keys[8], 3), WINDOW_ROWS // ROWS_DEV)
    route_ids = jax.vmap(lambda own, number: routed_block(jax.random.fold_in(part_keys[8], 2), own, number, ROWS_DEV, EXPERTS, TOPK, MOST, 2))(route_ids_keys, route_ids_turns).reshape((WINDOW_ROWS, TOPK))
    route_weights = jnp.clip(jnp.exp(math.log(1.0) - 2.9957323 * jax.random.uniform(part_keys[9], (WINDOW_ROWS, TOPK), jnp.float32) ** level_of(part_keys[9], (WINDOW_ROWS, TOPK), ((0, 16),), -0.2, 0.2)), 0.05, 1.0)
    placement = jax.random.permutation(key_list[10], EXPERTS).astype(jnp.int32)
    return dict(queries=queries, fresh_key_value=fresh_key_value, cache_key_value=cache_key_value, residual=residual, norm_gain=norm_gain, out_proj=out_proj, w_gate_up=w_gate_up, w_down=w_down, route_ids=route_ids, route_weights=route_weights, placement=placement)


def reference(queries, fresh_key_value, cache_key_value, residual, norm_gain, out_proj, w_gate_up, w_down, route_ids, route_weights, placement):
    count_of_rows = queries.shape[0]
    query_group_width = QUERY_HEADS // KEY_VALUE_HEADS
    scale_for_scores = HEAD_SIZE ** (-0.5)
    stored_keys = cache_key_value[0].astype(jnp.float32).reshape(-1, KEY_VALUE_HEADS, HEAD_SIZE)
    stored_values = cache_key_value[1].astype(jnp.float32).reshape(-1, KEY_VALUE_HEADS, HEAD_SIZE)
    block_of_rows = math.gcd(count_of_rows, 128)

    def attend(pieces):
        block_of_queries, self_key, self_value = pieces
        widened_query = block_of_queries.astype(jnp.float32).reshape(block_of_rows, KEY_VALUE_HEADS, query_group_width, HEAD_SIZE)
        scores = jnp.einsum('rkgd,jkd->rkgj', widened_query, stored_keys) * scale_for_scores
        self_score = jnp.einsum('ejaz,ejz->eja', widened_query, self_key.astype(jnp.float32).reshape(block_of_rows, KEY_VALUE_HEADS, HEAD_SIZE)) * scale_for_scores
        peak_value = jnp.maximum(lax.optimization_barrier(jnp.max(scores, axis=-1)), self_score)
        weights = jnp.exp(scores - peak_value[..., None])
        self_weight = jnp.exp(self_score - peak_value)
        totals = lax.optimization_barrier(jnp.sum(weights, axis=-1)) + self_weight
        weighted_total = jnp.einsum('rkgj,jkd->rkgd', weights.astype(jnp.bfloat16).astype(jnp.float32), stored_values)
        weighted_total = weighted_total + self_weight[..., None] * self_value.astype(jnp.float32).reshape(block_of_rows, KEY_VALUE_HEADS, 1, HEAD_SIZE)
        return (weighted_total / totals[..., None]).reshape(block_of_rows, QUERY_HEADS * HEAD_SIZE).astype(jnp.bfloat16)

    def blocked(array):
        return array.reshape(count_of_rows // block_of_rows, block_of_rows, array.shape[-1])
    attention = lax.map(attend, (blocked(queries), blocked(fresh_key_value[0]), blocked(fresh_key_value[1]))).reshape(count_of_rows, QUERY_HEADS * HEAD_SIZE)
    projected = jnp.dot(attention, out_proj, preferred_element_type=jnp.float32)
    hidden = (residual.astype(jnp.float32) + projected).astype(jnp.bfloat16)
    hidden_wide = hidden.astype(jnp.float32)
    normed = (hidden_wide * lax.rsqrt(lax.optimization_barrier(jnp.mean(hidden_wide * hidden_wide, axis=-1, keepdims=True)) + 1e-06) * norm_gain).astype(jnp.bfloat16)
    expert_count = placement.shape[0]
    slot_ids = placement[route_ids].reshape(-1).astype(jnp.int32)
    assigned = slot_ids.shape[0]
    sorted_idx = jnp.argsort(slot_ids, stable=True).astype(jnp.int32)
    expert_range = jnp.arange(expert_count, dtype=jnp.int32)
    counts = lax.optimization_barrier(jnp.sum((slot_ids[:, None] == expert_range[None, :]).astype(jnp.int32), axis=0)).astype(jnp.int32)
    starts = (jnp.cumsum(counts) - counts).astype(jnp.int32)
    capacity = N_CTX * MOST
    offsets = jnp.arange(capacity, dtype=jnp.int32)
    picked = jnp.minimum(starts[:, None] + offsets[None, :], assigned - 1).astype(jnp.int32)
    filled = offsets[None, :] < counts[:, None]
    source_rows = (sorted_idx[picked] // TOPK).astype(jnp.int32)

    def expert_run(pieces):
        slot_index, row_index, keep_rows = pieces
        inputs = jnp.where(keep_rows[:, None], normed[row_index], jnp.zeros((), jnp.bfloat16))
        both = jnp.dot(inputs, w_gate_up[slot_index], preferred_element_type=jnp.float32)
        active = (jax.nn.silu(both[:, :FF]) * both[:, FF:]).astype(jnp.bfloat16)
        return jnp.dot(active, w_down[slot_index], preferred_element_type=jnp.float32).astype(jnp.bfloat16)
    results = lax.map(expert_run, (expert_range, source_rows, filled))
    ranks = jnp.zeros((assigned,), jnp.int32).at[sorted_idx].set(jnp.arange(assigned, dtype=jnp.int32) - starts[slot_ids[sorted_idx]])
    routed = results[slot_ids, ranks].reshape(count_of_rows, TOPK, D).astype(jnp.float32)
    gate_share = route_weights / lax.optimization_barrier(jnp.sum(route_weights, axis=-1, keepdims=True))
    expert_out = lax.optimization_barrier(jnp.sum(gate_share[..., None] * routed, axis=1)).astype(jnp.bfloat16)
    return (hidden, expert_out)
```

```python
import functools

import jax
import jax.numpy as jnp
from jax import lax
from jax.experimental import pallas as pl
from jax.experimental.pallas import tpu as pltpu
from jax.sharding import PartitionSpec as P

D = 2048
QUERY_HEADS = 32
KEY_VALUE_HEADS = 4
HEAD_SIZE = 128
FF = 768
TOPK = 8
HEADS_STEP = 4

epsilon = 1e-06

VMEM = pl.BlockSpec(memory_space=pltpu.VMEM)
RIGHT, LEFT = 0, 1


def chip_at(q, m):
    return jnp.where(q < m // 2, 2 * q, 2 * (m - 1 - q) + 1)


def place_of(chip, m):
    return jnp.where(chip % 2 == 0, chip // 2, m - 1 - chip // 2)


def ring(m):
    me = lax.axis_index("ctx")
    core, p = me % 2, place_of(me // 2, m)

    def at(offset, c):
        return chip_at((p + offset + m) % m, m) * 2 + c

    return me, core, at


def greet(others):
    barrier = pltpu.get_barrier_semaphore()
    for other in others:
        pl.semaphore_signal(
            barrier, inc=1, device_id={"ctx": other}, device_id_type=pl.DeviceIdType.MESH
        )
    pl.semaphore_wait(barrier, len(others))


def remote(src, dst, send, recv, other):
    return pltpu.make_async_remote_copy(
        src_ref=src,
        dst_ref=dst,
        send_sem=send,
        recv_sem=recv,
        device_id={"ctx": other},
        device_id_type=pl.DeviceIdType.MESH,
    )


def travels(way, half, d, reach):
    return d < reach or (d == reach and half == way)


PAIRS = ((RIGHT, 0), (LEFT, 1), (RIGHT, 1), (LEFT, 0))


def gather_kernel(n, x_ref, out_ref, ring_send, ring_recv, mate_send, mate_recv):
    m, reach = n // 2, n // 4
    me, core, at = ring(m)
    mate = at(0, 1 - core)
    neighbour = (at(1, core), at(-1, core))
    half_width = x_ref.shape[1] // 2
    cols = [pl.ds(h * half_width, half_width) for h in range(2)]
    greet((neighbour[0], neighbour[1], mate))
    started = []

    def forward(src, owner, way, half, d):
        copy = remote(
            src,
            out_ref.at[owner, :, cols[half]],
            ring_send.at[way, d, half],
            ring_recv.at[way, d, half],
            neighbour[way],
        )
        copy.start()
        started.append(copy)

    for way, half in PAIRS:
        forward(x_ref.at[:, cols[half]], me, way, half, 0)
    copy = remote(x_ref, out_ref.at[me], mate_send.at[0, 0, 0], mate_recv.at[0, 0, 0], mate)
    copy.start()
    started.append(copy)
    out_ref[me] = x_ref[...]
    for d in range(1, reach + 1):
        for way, half in PAIRS:
            if not travels(way, half, d, reach):
                continue
            owner = at(-d if way == RIGHT else d, core)
            piece = out_ref.at[owner, :, cols[half]]
            remote(
                piece, piece, ring_send.at[way, d - 1, half], ring_recv.at[way, d - 1, half], mate
            ).wait_recv()
            if travels(way, half, d + 1, reach):
                forward(piece, owner, way, half, d)
            copy = remote(
                piece, piece, mate_send.at[way, d, half], mate_recv.at[way, d, half], mate
            )
            copy.start()
            started.append(copy)
    theirs = out_ref.at[mate]
    remote(theirs, theirs, mate_send.at[0, 0, 0], mate_recv.at[0, 0, 0], mate).wait_recv()
    for d in range(1, reach + 1):
        for way, half in PAIRS:
            if travels(way, half, d, reach):
                owner = at(-d if way == RIGHT else d, 1 - core)
                piece = out_ref.at[owner, :, cols[half]]
                remote(
                    piece, piece, mate_send.at[way, d, half], mate_recv.at[way, d, half], mate
                ).wait_recv()
    for copy in started:
        copy.wait_send()


def ring_gather(x, n, collective_id):
    reach = n // 4
    return pl.pallas_call(
        functools.partial(gather_kernel, n),
        out_shape=jax.ShapeDtypeStruct((n,) + x.shape, x.dtype),
        in_specs=[VMEM],
        out_specs=VMEM,
        scratch_shapes=[
            pltpu.SemaphoreType.DMA((2, reach, 2)),
            pltpu.SemaphoreType.DMA((2, reach, 2)),
            pltpu.SemaphoreType.DMA((2, reach + 1, 2)),
            pltpu.SemaphoreType.DMA((2, reach + 1, 2)),
        ],
        compiler_params=pltpu.CompilerParams(collective_id=collective_id, has_side_effects=True),
        name=f"gather{collective_id}",
    )(x)


def scatter_kernel(
    n,
    x_ref,
    out_ref,
    from_mate,
    outgoing,
    incoming,
    ring_send,
    ring_recv,
    mate_send,
    mate_recv,
):
    m, reach = n // 2, n // 4
    me, core, at = ring(m)
    mate = at(0, 1 - core)
    neighbour = (at(1, core), at(-1, core))
    half_width = x_ref.shape[2] // 2
    cols = [pl.ds(h * half_width, half_width) for h in range(2)]
    greet((neighbour[0], neighbour[1], mate))
    started = []
    offsets = [reach]
    for d in range(reach - 1, 0, -1):
        offsets += [d, -d]
    offsets.append(0)
    mate_copies = []
    for k, offset in enumerate(offsets):
        copy = remote(
            x_ref.at[at(offset, 1 - core)],
            from_mate.at[k],
            mate_send.at[k],
            mate_recv.at[k],
            mate,
        )
        copy.start()
        started.append(copy)
        mate_copies.append(copy)
    arrived = set()

    def chip_sum(offset, half):
        k = offsets.index(offset)
        if k not in arrived:
            mate_copies[k].wait_recv()
            arrived.add(k)
        mine = x_ref[at(offset, core), :, cols[half]].astype(jnp.float32)
        return mine + from_mate[k, :, cols[half]].astype(jnp.float32)

    def received(way, half, d):
        piece = incoming.at[way, d, half]
        remote(
            piece, piece, ring_send.at[way, d, half], ring_recv.at[way, d, half], mate
        ).wait_recv()
        return incoming[way, d, half].astype(jnp.float32)

    for d in range(reach, 0, -1):
        for way, half in ((RIGHT, 1), (LEFT, 0), (RIGHT, 0), (LEFT, 1)):
            if not travels(way, half, d, reach):
                continue
            offset = d if (way == RIGHT or d == reach) else -d
            total = chip_sum(offset, half)
            if travels(way, half, d + 1, reach):
                total = total + received(way, half, d)
            outgoing[way, d - 1, half] = total.astype(jnp.bfloat16)
            copy = remote(
                outgoing.at[way, d - 1, half],
                incoming.at[way, d - 1, half],
                ring_send.at[way, d - 1, half],
                ring_recv.at[way, d - 1, half],
                neighbour[way],
            )
            copy.start()
            started.append(copy)
    for half in range(2):
        total = chip_sum(0, half) + received(RIGHT, half, 0) + received(LEFT, half, 0)
        out_ref[:, cols[half]] = total
    for copy in started:
        copy.wait_send()


def ring_scatter(x, n, collective_id):
    m, reach = n // 2, n // 4
    rows, width = x.shape[1:]
    piece = (2, reach, 2, rows, width // 2)
    return pl.pallas_call(
        functools.partial(scatter_kernel, n),
        out_shape=jax.ShapeDtypeStruct((rows, width), jnp.float32),
        in_specs=[VMEM],
        out_specs=VMEM,
        scratch_shapes=[
            pltpu.VMEM((m, rows, width), jnp.bfloat16),
            pltpu.VMEM(piece, jnp.bfloat16),
            pltpu.VMEM(piece, jnp.bfloat16),
            pltpu.SemaphoreType.DMA((2, reach, 2)),
            pltpu.SemaphoreType.DMA((2, reach, 2)),
            pltpu.SemaphoreType.DMA((m,)),
            pltpu.SemaphoreType.DMA((m,)),
        ],
        compiler_params=pltpu.CompilerParams(collective_id=collective_id, has_side_effects=True),
        name=f"scatter{collective_id}",
    )(x)


def exchange_kernel(n, x_ref, out_ref, send, recv):
    me = lax.axis_index("ctx")
    greet([(me + j) % n for j in range(1, n)])
    copies = []
    for j in range(1, n):
        other = (me + j) % n
        copy = remote(x_ref.at[other], out_ref.at[me], send.at[j], recv.at[j], other)
        copy.start()
        copies.append(copy)
    out_ref[me] = x_ref[me]
    for j in range(1, n):
        source = (me + n - j) % n
        piece = out_ref.at[source]
        remote(piece, piece, send.at[j], recv.at[j], source).wait_recv()
    for copy in copies:
        copy.wait_send()


def exchange(x, n, collective_id):
    return pl.pallas_call(
        functools.partial(exchange_kernel, n),
        out_shape=jax.ShapeDtypeStruct(x.shape, x.dtype),
        in_specs=[VMEM],
        out_specs=VMEM,
        scratch_shapes=[pltpu.SemaphoreType.DMA((n,)), pltpu.SemaphoreType.DMA((n,))],
        compiler_params=pltpu.CompilerParams(collective_id=collective_id, has_side_effects=True),
        name=f"exchange{collective_id}",
    )(x)


def attend_kernel(per, q_ref, fresh_key_ref, fresh_value_ref, key_ref, value_ref, out_ref):
    rows = q_ref.shape[0]
    keys = key_ref[...].reshape(-1, HEAD_SIZE)
    values = value_ref[...].reshape(-1, HEAD_SIZE)
    fresh_key = fresh_key_ref[...].astype(jnp.float32)
    fresh_value = fresh_value_ref[...].astype(jnp.float32)
    scale = HEAD_SIZE ** (-0.5)
    heads = [q_ref[:, h * HEAD_SIZE : (h + 1) * HEAD_SIZE] for h in range(HEADS_STEP)]
    scores = (
        lax.dot_general(
            jnp.concatenate(heads, axis=0),
            keys,
            (((1,), (1,)), ((), ())),
            preferred_element_type=jnp.float32,
        )
        * scale
    )
    own = jnp.concatenate(
        [jnp.sum(q.astype(jnp.float32) * fresh_key, axis=-1, keepdims=True) for q in heads], axis=0
    )
    own = own * scale
    peak = jnp.maximum(own, jnp.max(scores, axis=-1, keepdims=True))
    weights = jnp.exp(scores - peak)
    own = jnp.exp(own - peak)
    totals = jnp.sum(weights, axis=-1, keepdims=True) + own
    mixed = jnp.dot(weights.astype(jnp.bfloat16), values, preferred_element_type=jnp.float32)
    for h in range(HEADS_STEP):
        part = slice(h * rows, (h + 1) * rows)
        result = (mixed[part] + own[part] * fresh_value) / totals[part]
        column = (h % per) * HEAD_SIZE
        out_ref[h // per, :, column : column + HEAD_SIZE] = result.astype(jnp.bfloat16)


def attend(queries, fresh_key_value, gathered, key_count, n):
    rows = queries.shape[0]
    per = QUERY_HEADS // n
    parts = QUERY_HEADS // KEY_VALUE_HEADS // HEADS_STEP
    fresh = lambda i: pl.BlockSpec((None, rows, HEAD_SIZE), lambda g, s, i=i: (i, 0, g))
    cached = lambda i: pl.BlockSpec((n, key_count, HEAD_SIZE), lambda g, s, i=i: (0, i, g))
    return pl.pallas_call(
        functools.partial(attend_kernel, per),
        grid=(KEY_VALUE_HEADS, parts),
        out_shape=jax.ShapeDtypeStruct((n, rows, per * HEAD_SIZE), jnp.bfloat16),
        in_specs=[
            pl.BlockSpec((rows, HEADS_STEP * HEAD_SIZE), lambda g, s: (0, g * parts + s)),
            fresh(0),
            fresh(1),
            cached(0),
            cached(1),
        ],
        out_specs=pl.BlockSpec(
            (HEADS_STEP // per, rows, per * HEAD_SIZE), lambda g, s: (g * parts + s, 0, 0)
        ),
        name="attend",
    )(queries, fresh_key_value, fresh_key_value, gathered, gathered)


def local(
    n,
    queries,
    fresh_key_value,
    cache_key_value,
    residual,
    norm_gain,
    out_proj,
    w_gate_up,
    w_down,
    route_ids,
    route_weights,
    placement,
):
    rows = queries.shape[0]
    expert_count = placement.shape[0]
    local_count = w_gate_up.shape[0]
    key_count = cache_key_value.shape[1]
    kv_width = cache_key_value.shape[2]
    capacity = n * max(2, 3 * rows * TOPK // (2 * expert_count))

    gate_share = route_weights / jnp.sum(route_weights, axis=-1, keepdims=True)
    slots = jnp.sum(
        jnp.where(route_ids[..., None] == jnp.arange(expert_count), placement, 0), axis=-1
    )
    slot_lanes = -(-expert_count // 128) * 128
    shares = jnp.sum(
        jnp.where(slots[..., None] == jnp.arange(slot_lanes), gate_share[..., None], 0.0), axis=1
    ).astype(jnp.bfloat16)
    share_rows = rows * slot_lanes // kv_width
    padded = -(-share_rows // 16) * 16
    packed = jnp.concatenate(
        [
            cache_key_value.reshape(2 * key_count, kv_width),
            jnp.pad(shares.reshape(share_rows, kv_width), ((0, padded - share_rows), (0, 0))),
        ],
        axis=0,
    )
    gathered = ring_gather(packed, n, 0)

    mine = lax.axis_index("ctx") * local_count
    all_shares = gathered[:, 2 * key_count : 2 * key_count + share_rows].reshape(
        n * rows, slot_lanes
    )
    my_shares = lax.dynamic_slice(all_shares, (0, mine), (n * rows, local_count)).T
    named = my_shares > 0
    ranks = jnp.cumsum(named.astype(jnp.int32), axis=1) - 1
    ranks = jnp.where(named, ranks, -1)
    chosen = ranks[:, None, :] == jnp.arange(capacity)[None, :, None]
    pick = chosen.astype(jnp.bfloat16).reshape(local_count * capacity, n * rows)
    spread = jnp.where(chosen, my_shares[:, None, :], jnp.zeros((), jnp.bfloat16)).reshape(
        local_count * capacity, n * rows
    )

    attention = exchange(attend(queries, fresh_key_value, gathered, key_count, n), n, 1)
    projected = jnp.dot(
        attention.reshape(n * rows, -1), out_proj, preferred_element_type=jnp.float32
    ).astype(jnp.bfloat16)
    projected = ring_scatter(projected.reshape(n, rows, D), n, 2)
    hidden = (residual.astype(jnp.float32) + projected).astype(jnp.bfloat16)
    hidden_wide = hidden.astype(jnp.float32)
    normed = (
        hidden_wide
        * lax.rsqrt(jnp.mean(hidden_wide * hidden_wide, axis=-1, keepdims=True) + epsilon)
        * norm_gain
    ).astype(jnp.bfloat16)
    all_normed = ring_gather(normed, n, 3).reshape(n * rows, D)

    inputs = (
        jnp.dot(pick, all_normed, preferred_element_type=jnp.float32)
        .astype(jnp.bfloat16)
        .reshape(local_count, capacity, D)
    )
    both = jnp.einsum("emd,edf->emf", inputs, w_gate_up, preferred_element_type=jnp.float32)
    active = (jax.nn.silu(both[..., :FF]) * both[..., FF:]).astype(jnp.bfloat16)
    produced = jnp.einsum(
        "emf,efd->emd", active, w_down, preferred_element_type=jnp.float32
    ).astype(jnp.bfloat16)
    combined = lax.dot_general(
        spread,
        produced.reshape(local_count * capacity, D),
        (((0,), (0,)), ((), ())),
        preferred_element_type=jnp.float32,
    ).astype(jnp.bfloat16)
    expert_out = ring_scatter(combined.reshape(n, rows, D), n, 4).astype(jnp.bfloat16)
    return (hidden, expert_out)


def solution(mesh):
    in_specs = (
        P(("groups", "ctx"), None),
        P(None, ("groups", "ctx"), None),
        P(None, ("groups", "ctx"), None),
        P(("groups", "ctx"), None),
        P(),
        P("ctx", None),
        P("ctx", None, None),
        P("ctx", None, None),
        P(("groups", "ctx"), None),
        P(("groups", "ctx"), None),
        P(),
    )
    out_specs = (P(("groups", "ctx"), None), P(("groups", "ctx"), None))
    return jax.shard_map(
        functools.partial(local, mesh.shape["ctx"]),
        mesh=mesh,
        in_specs=in_specs,
        out_specs=out_specs,
        check_vma=False,
    )
```

```python
import functools

import jax
import jax.numpy as jnp
from jax import lax
from jax.experimental import pallas as pl
from jax.experimental.pallas import tpu as pltpu
from jax.sharding import PartitionSpec as P

D = 2048
QUERY_HEADS = 32
KEY_VALUE_HEADS = 4
HEAD_SIZE = 128
FF = 768
TOPK = 8
HEADS_STEP = 4
COLUMNS_STEP = 512

epsilon = 1e-06

VMEM = pl.BlockSpec(memory_space=pltpu.VMEM)
RIGHT, LEFT = 0, 1


def chip_at(q, m):
    return jnp.where(q < m // 2, 2 * q, 2 * (m - 1 - q) + 1)


def place_of(chip, m):
    return jnp.where(chip % 2 == 0, chip // 2, m - 1 - chip // 2)


def ring(m):
    me = lax.axis_index("ctx")
    core, p = me % 2, place_of(me // 2, m)

    def at(offset, c):
        return chip_at((p + offset + m) % m, m) * 2 + c

    return me, core, at


def greet(others):
    barrier = pltpu.get_barrier_semaphore()
    for other in others:
        pl.semaphore_signal(
            barrier, inc=1, device_id={"ctx": other}, device_id_type=pl.DeviceIdType.MESH
        )
    pl.semaphore_wait(barrier, len(others))


def remote(src, dst, send, recv, other):
    return pltpu.make_async_remote_copy(
        src_ref=src,
        dst_ref=dst,
        send_sem=send,
        recv_sem=recv,
        device_id={"ctx": other},
        device_id_type=pl.DeviceIdType.MESH,
    )


def travels(way, half, d, reach):
    return d < reach or (d == reach and half == way)


PAIRS = ((RIGHT, 0), (LEFT, 1), (RIGHT, 1), (LEFT, 0))


def gather_kernel(n, x_ref, out_ref, ring_send, ring_recv, mate_send, mate_recv):
    m, reach = n // 2, n // 4
    me, core, at = ring(m)
    mate = at(0, 1 - core)
    neighbour = (at(1, core), at(-1, core))
    half_width = x_ref.shape[1] // 2
    cols = [pl.ds(h * half_width, half_width) for h in range(2)]
    greet((neighbour[0], neighbour[1], mate))
    started = []

    def forward(src, owner, way, half, d):
        copy = remote(
            src,
            out_ref.at[owner, :, cols[half]],
            ring_send.at[way, d, half],
            ring_recv.at[way, d, half],
            neighbour[way],
        )
        copy.start()
        started.append(copy)

    for way, half in PAIRS:
        forward(x_ref.at[:, cols[half]], me, way, half, 0)
    copy = remote(x_ref, out_ref.at[me], mate_send.at[0, 0, 0], mate_recv.at[0, 0, 0], mate)
    copy.start()
    started.append(copy)
    out_ref[me] = x_ref[...]
    for d in range(1, reach + 1):
        for way, half in PAIRS:
            if not travels(way, half, d, reach):
                continue
            owner = at(-d if way == RIGHT else d, core)
            piece = out_ref.at[owner, :, cols[half]]
            remote(
                piece, piece, ring_send.at[way, d - 1, half], ring_recv.at[way, d - 1, half], mate
            ).wait_recv()
            if travels(way, half, d + 1, reach):
                forward(piece, owner, way, half, d)
            copy = remote(
                piece, piece, mate_send.at[way, d, half], mate_recv.at[way, d, half], mate
            )
            copy.start()
            started.append(copy)
    theirs = out_ref.at[mate]
    remote(theirs, theirs, mate_send.at[0, 0, 0], mate_recv.at[0, 0, 0], mate).wait_recv()
    for d in range(1, reach + 1):
        for way, half in PAIRS:
            if travels(way, half, d, reach):
                owner = at(-d if way == RIGHT else d, 1 - core)
                piece = out_ref.at[owner, :, cols[half]]
                remote(
                    piece, piece, mate_send.at[way, d, half], mate_recv.at[way, d, half], mate
                ).wait_recv()
    for copy in started:
        copy.wait_send()


def ring_gather(x, n, collective_id):
    reach = n // 4
    return pl.pallas_call(
        functools.partial(gather_kernel, n),
        out_shape=jax.ShapeDtypeStruct((n,) + x.shape, x.dtype),
        in_specs=[VMEM],
        out_specs=VMEM,
        scratch_shapes=[
            pltpu.SemaphoreType.DMA((2, reach, 2)),
            pltpu.SemaphoreType.DMA((2, reach, 2)),
            pltpu.SemaphoreType.DMA((2, reach + 1, 2)),
            pltpu.SemaphoreType.DMA((2, reach + 1, 2)),
        ],
        compiler_params=pltpu.CompilerParams(collective_id=collective_id, has_side_effects=True),
        name=f"gather{collective_id}",
    )(x)


def scatter_kernel(n, finish, extras, lhs_ref, rhs_ref, *refs):
    extra_refs, refs = refs[:extras], refs[extras:]
    outs, scratch = refs[:-8], refs[-8:]
    made, from_mate, outgoing, incoming, ring_send, ring_recv, mate_send, mate_recv = scratch
    m, reach = n // 2, n // 4
    me, core, at = ring(m)
    mate = at(0, 1 - core)
    neighbour = (at(1, core), at(-1, core))
    rows, width = made.shape[2:]
    half_width = width // 2
    cols = [pl.ds(h * half_width, half_width) for h in range(2)]
    greet((neighbour[0], neighbour[1], mate))
    started = []
    offsets = [reach]
    for d in range(reach - 1, 0, -1):
        offsets += [d, -d]
    offsets.append(0)
    mate_copies = {}

    def make(offset):
        k = offsets.index(offset)
        lhs = lhs_ref.at[at(offset, 0) // 2]

        @pl.loop(0, width // COLUMNS_STEP)
        def _(c):
            part = pl.ds(pl.multiple_of(c * COLUMNS_STEP, COLUMNS_STEP), COLUMNS_STEP)
            product = jnp.dot(lhs[...], rhs_ref[:, part], preferred_element_type=jnp.float32)
            product = product.astype(jnp.bfloat16)
            made[k, 0, :, part] = product[:rows]
            made[k, 1, :, part] = product[rows:]

        copy = remote(
            made.at[k, 1 - core], from_mate.at[k], mate_send.at[k], mate_recv.at[k], mate
        )
        copy.start()
        started.append(copy)
        mate_copies[k] = copy

    def make_level(d):
        for offset in offsets:
            if abs(offset) == d:
                make(offset)

    arrived = set()

    def chip_sum(offset, half):
        k = offsets.index(offset)
        if k not in arrived:
            mate_copies[k].wait_recv()
            arrived.add(k)
        mine = made[k, core, :, cols[half]].astype(jnp.float32)
        return mine + from_mate[k, :, cols[half]].astype(jnp.float32)

    def received(way, half, d):
        piece = incoming.at[way, d, half]
        remote(
            piece, piece, ring_send.at[way, d, half], ring_recv.at[way, d, half], mate
        ).wait_recv()
        return incoming[way, d, half].astype(jnp.float32)

    make_level(reach)
    for d in range(reach, 0, -1):
        make_level(d - 1)
        for way, half in ((RIGHT, 1), (LEFT, 0), (RIGHT, 0), (LEFT, 1)):
            if not travels(way, half, d, reach):
                continue
            offset = d if (way == RIGHT or d == reach) else -d
            total = chip_sum(offset, half)
            if travels(way, half, d + 1, reach):
                total = total + received(way, half, d)
            outgoing[way, d - 1, half] = total.astype(jnp.bfloat16)
            copy = remote(
                outgoing.at[way, d - 1, half],
                incoming.at[way, d - 1, half],
                ring_send.at[way, d - 1, half],
                ring_recv.at[way, d - 1, half],
                neighbour[way],
            )
            copy.start()
            started.append(copy)
    totals = [
        chip_sum(0, half) + received(RIGHT, half, 0) + received(LEFT, half, 0) for half in range(2)
    ]
    finish(totals, cols, extra_refs, outs)
    for copy in started:
        copy.wait_send()


def finish_plain(totals, cols, extra_refs, outs):
    for half in range(2):
        outs[0][:, cols[half]] = totals[half].astype(jnp.bfloat16)


def finish_normed(totals, cols, extra_refs, outs):
    residual_ref, gain_ref = extra_refs
    hidden_ref, normed_ref = outs
    squares = 0.0
    for half in range(2):
        hidden = totals[half] + residual_ref[:, cols[half]].astype(jnp.float32)
        hidden = hidden.astype(jnp.bfloat16)
        hidden_ref[:, cols[half]] = hidden
        wide = hidden.astype(jnp.float32)
        squares = squares + jnp.sum(wide * wide, axis=-1, keepdims=True)
    scale = lax.rsqrt(squares / hidden_ref.shape[1] + epsilon)
    for half in range(2):
        wide = hidden_ref[:, cols[half]].astype(jnp.float32)
        normed_ref[:, cols[half]] = (wide * scale * gain_ref[:, cols[half]]).astype(jnp.bfloat16)


def ring_scatter(lhs, rhs, n, collective_id, finish=finish_plain, extras=(), outputs=1):
    m, reach = n // 2, n // 4
    rows, width = lhs.shape[1] // 2, rhs.shape[1]
    piece = (2, reach, 2, rows, width // 2)
    return pl.pallas_call(
        functools.partial(scatter_kernel, n, finish, len(extras)),
        out_shape=[jax.ShapeDtypeStruct((rows, width), jnp.bfloat16)] * outputs,
        in_specs=[VMEM] * (2 + len(extras)),
        out_specs=[VMEM] * outputs,
        scratch_shapes=[
            pltpu.VMEM((m, 2, rows, width), jnp.bfloat16),
            pltpu.VMEM((m, rows, width), jnp.bfloat16),
            pltpu.VMEM(piece, jnp.bfloat16),
            pltpu.VMEM(piece, jnp.bfloat16),
            pltpu.SemaphoreType.DMA((2, reach, 2)),
            pltpu.SemaphoreType.DMA((2, reach, 2)),
            pltpu.SemaphoreType.DMA((m,)),
            pltpu.SemaphoreType.DMA((m,)),
        ],
        compiler_params=pltpu.CompilerParams(collective_id=collective_id, has_side_effects=True),
        name=f"scatter{collective_id}",
    )(lhs, rhs, *extras)


def attend_kernel(n, key_count, q_ref, fresh_ref, cached_ref, out_ref, stage, send, recv):
    me = lax.axis_index("ctx")
    rows = q_ref.shape[0]
    per = QUERY_HEADS // n
    group = HEADS_STEP // per
    steps = n // group
    scale = HEAD_SIZE ** (-0.5)
    greet([(me + j) % n for j in range(1, n)])

    def heads_of(u):
        pair = u * HEADS_STEP // (QUERY_HEADS // KEY_VALUE_HEADS)
        lanes = pl.ds(pl.multiple_of(pair * HEAD_SIZE, HEAD_SIZE), HEAD_SIZE)
        keys = cached_ref[:, :key_count, lanes].reshape(-1, HEAD_SIZE)
        values = cached_ref[:, key_count : 2 * key_count, lanes].reshape(-1, HEAD_SIZE)
        fresh_key = fresh_ref[0, :, lanes].astype(jnp.float32)
        fresh_value = fresh_ref[1, :, lanes].astype(jnp.float32)
        width = HEADS_STEP * HEAD_SIZE
        block = q_ref[:, pl.ds(pl.multiple_of(u * width, width), width)]
        heads = [block[:, h * HEAD_SIZE : (h + 1) * HEAD_SIZE] for h in range(HEADS_STEP)]
        scores = (
            lax.dot_general(
                jnp.concatenate(heads, axis=0),
                keys,
                (((1,), (1,)), ((), ())),
                preferred_element_type=jnp.float32,
            )
            * scale
        )
        own = jnp.concatenate(
            [jnp.sum(q.astype(jnp.float32) * fresh_key, axis=-1, keepdims=True) for q in heads],
            axis=0,
        )
        own = own * scale
        peak = jnp.maximum(own, jnp.max(scores, axis=-1, keepdims=True))
        weights = jnp.exp(scores - peak)
        own = jnp.exp(own - peak)
        totals = jnp.sum(weights, axis=-1, keepdims=True) + own
        mixed = jnp.dot(weights.astype(jnp.bfloat16), values, preferred_element_type=jnp.float32)
        for h in range(HEADS_STEP):
            part = slice(h * rows, (h + 1) * rows)
            result = (mixed[part] + own[part] * fresh_value) / totals[part]
            column = (h % per) * HEAD_SIZE
            stage[u * group + h // per, :, column : column + HEAD_SIZE] = result.astype(
                jnp.bfloat16
            )

    def copy_to(other):
        return remote(stage.at[other], out_ref.at[me], send.at[other], recv.at[me], other)

    @pl.loop(0, steps - 1)
    def _(s):
        u = (me // group + 1 + s) % steps
        heads_of(u)
        for j in range(group):
            copy_to(u * group + j).start()

    heads_of(me // group)
    near = [me // group * group + (me % group + j) % group for j in range(1, group)]
    for other in near:
        copy_to(other).start()
    out_ref[me] = stage[me]
    for j in range(1, n):
        source = (me + n - j) % n
        piece = out_ref.at[source]
        remote(piece, piece, send.at[source], recv.at[source], source).wait_recv()
    for j in range(1, n):
        copy_to((me + j) % n).wait_send()


def attend(queries, fresh_key_value, gathered, key_count, n, collective_id):
    rows = queries.shape[0]
    shape = (n, rows, QUERY_HEADS // n * HEAD_SIZE)
    return pl.pallas_call(
        functools.partial(attend_kernel, n, key_count),
        out_shape=jax.ShapeDtypeStruct(shape, jnp.bfloat16),
        in_specs=[VMEM] * 3,
        out_specs=VMEM,
        scratch_shapes=[
            pltpu.VMEM(shape, jnp.bfloat16),
            pltpu.SemaphoreType.DMA((n,)),
            pltpu.SemaphoreType.DMA((n,)),
        ],
        compiler_params=pltpu.CompilerParams(collective_id=collective_id, has_side_effects=True),
        name="attend",
    )(queries, fresh_key_value, gathered)


def local(
    n,
    queries,
    fresh_key_value,
    cache_key_value,
    residual,
    norm_gain,
    out_proj,
    w_gate_up,
    w_down,
    route_ids,
    route_weights,
    placement,
):
    rows = queries.shape[0]
    expert_count = placement.shape[0]
    local_count = w_gate_up.shape[0]
    key_count = cache_key_value.shape[1]
    kv_width = cache_key_value.shape[2]
    capacity = n * max(2, 3 * rows * TOPK // (2 * expert_count))

    gate_share = route_weights / jnp.sum(route_weights, axis=-1, keepdims=True)
    slots = jnp.sum(
        jnp.where(route_ids[..., None] == jnp.arange(expert_count), placement, 0), axis=-1
    )
    slot_lanes = -(-expert_count // 128) * 128
    shares = jnp.sum(
        jnp.where(slots[..., None] == jnp.arange(slot_lanes), gate_share[..., None], 0.0), axis=1
    ).astype(jnp.bfloat16)
    share_rows = rows * slot_lanes // kv_width
    padded = -(-share_rows // 16) * 16
    packed = jnp.concatenate(
        [
            cache_key_value.reshape(2 * key_count, kv_width),
            jnp.pad(shares.reshape(share_rows, kv_width), ((0, padded - share_rows), (0, 0))),
        ],
        axis=0,
    )
    gathered = ring_gather(packed, n, 0)

    mine = lax.axis_index("ctx") * local_count
    all_shares = gathered[:, 2 * key_count : 2 * key_count + share_rows].reshape(
        n * rows, slot_lanes
    )
    my_shares = lax.dynamic_slice(all_shares, (0, mine), (n * rows, local_count)).T
    named = my_shares > 0
    ranks = jnp.cumsum(named.astype(jnp.int32), axis=1) - 1
    ranks = jnp.where(named, ranks, -1)
    chosen = ranks[:, None, :] == jnp.arange(capacity)[None, :, None]
    pick = chosen.astype(jnp.bfloat16).reshape(local_count * capacity, n * rows)
    spread = jnp.where(
        ranks.T[:, :, None] == jnp.arange(capacity), my_shares.T[:, :, None], jnp.zeros((), jnp.bfloat16)
    ).reshape(n * rows, local_count * capacity)

    attention = attend(queries, fresh_key_value, gathered, key_count, n, 1)
    hidden, normed = ring_scatter(
        attention.reshape(n // 2, 2 * rows, -1),
        out_proj,
        n,
        2,
        finish_normed,
        (residual, norm_gain.reshape(1, D)),
        2,
    )
    all_normed = ring_gather(normed, n, 3).reshape(n * rows, D)

    inputs = (
        jnp.dot(pick, all_normed, preferred_element_type=jnp.float32)
        .astype(jnp.bfloat16)
        .reshape(local_count, capacity, D)
    )
    both = jnp.einsum("emd,edf->emf", inputs, w_gate_up, preferred_element_type=jnp.float32)
    active = (jax.nn.silu(both[..., :FF]) * both[..., FF:]).astype(jnp.bfloat16)
    produced = jnp.einsum(
        "emf,efd->emd", active, w_down, preferred_element_type=jnp.float32
    ).astype(jnp.bfloat16)
    (expert_out,) = ring_scatter(
        spread.reshape(n // 2, 2 * rows, -1), produced.reshape(local_count * capacity, D), n, 4
    )
    return (hidden, expert_out)


def solution(mesh):
    in_specs = (
        P(("groups", "ctx"), None),
        P(None, ("groups", "ctx"), None),
        P(None, ("groups", "ctx"), None),
        P(("groups", "ctx"), None),
        P(),
        P("ctx", None),
        P("ctx", None, None),
        P("ctx", None, None),
        P(("groups", "ctx"), None),
        P(("groups", "ctx"), None),
        P(),
    )
    out_specs = (P(("groups", "ctx"), None), P(("groups", "ctx"), None))
    return jax.shard_map(
        functools.partial(local, mesh.shape["ctx"]),
        mesh=mesh,
        in_specs=in_specs,
        out_specs=out_specs,
        check_vma=False,
    )
```

```python
import functools

import jax
import jax.numpy as jnp
from jax import lax
from jax.experimental import pallas as pl
from jax.experimental.pallas import tpu as pltpu
from jax.sharding import PartitionSpec as P

D = 2048
QUERY_HEADS = 32
KEY_VALUE_HEADS = 4
HEAD_SIZE = 128
FF = 768
TOPK = 8
HEADS_STEP = 4
COLUMNS_STEP = 512

epsilon = 1e-06

VMEM = pl.BlockSpec(memory_space=pltpu.VMEM)
RIGHT, LEFT = 0, 1


def chip_at(q, m):
    return jnp.where(q < m // 2, 2 * q, 2 * (m - 1 - q) + 1)


def place_of(chip, m):
    return jnp.where(chip % 2 == 0, chip // 2, m - 1 - chip // 2)


def ring(m):
    me = lax.axis_index("ctx")
    core, p = me % 2, place_of(me // 2, m)

    def at(offset, c):
        return chip_at((p + offset + m) % m, m) * 2 + c

    return me, core, at


def greet(others):
    barrier = pltpu.get_barrier_semaphore()
    for other in others:
        pl.semaphore_signal(
            barrier, inc=1, device_id={"ctx": other}, device_id_type=pl.DeviceIdType.MESH
        )
    pl.semaphore_wait(barrier, len(others))


def remote(src, dst, send, recv, other):
    return pltpu.make_async_remote_copy(
        src_ref=src,
        dst_ref=dst,
        send_sem=send,
        recv_sem=recv,
        device_id={"ctx": other},
        device_id_type=pl.DeviceIdType.MESH,
    )


def travels(way, half, d, reach):
    return d < reach or (d == reach and half == way)


PAIRS = ((RIGHT, 0), (LEFT, 1), (RIGHT, 1), (LEFT, 0))


def gather_kernel(n, x_ref, out_ref, ring_send, ring_recv, mate_send, mate_recv, work=None):
    m, reach = n // 2, n // 4
    me, core, at = ring(m)
    mate = at(0, 1 - core)
    neighbour = (at(1, core), at(-1, core))
    half_width = x_ref.shape[1] // 2
    cols = [pl.ds(h * half_width, half_width) for h in range(2)]
    greet((neighbour[0], neighbour[1], mate))
    started = []

    def forward(src, owner, way, half, d):
        copy = remote(
            src,
            out_ref.at[owner, :, cols[half]],
            ring_send.at[way, d, half],
            ring_recv.at[way, d, half],
            neighbour[way],
        )
        copy.start()
        started.append(copy)

    for way, half in PAIRS:
        forward(x_ref.at[:, cols[half]], me, way, half, 0)
    copy = remote(x_ref, out_ref.at[me], mate_send.at[0, 0, 0], mate_recv.at[0, 0, 0], mate)
    copy.start()
    started.append(copy)
    out_ref[me] = x_ref[...]
    def wait_mate(offset):
        if offset == 0:
            theirs = out_ref.at[mate]
            remote(theirs, theirs, mate_send.at[0, 0, 0], mate_recv.at[0, 0, 0], mate).wait_recv()
            return
        d = abs(offset)
        for way, half in PAIRS:
            if travels(way, half, d, reach) and (d == reach or (way == RIGHT) == (offset < 0)):
                piece = out_ref.at[at(offset, 1 - core), :, cols[half]]
                remote(
                    piece, piece, mate_send.at[way, d, half], mate_recv.at[way, d, half], mate
                ).wait_recv()

    def offsets_at(d):
        return [d] if d in (0, reach) else [-d, d]

    def jobs_at(d):
        jobs = []
        for offset in offsets_at(d):
            chip = at(offset, 0) // 2

            def first(offset=offset, chip=chip):
                wait_mate(offset)
                if work is not None:
                    work(chip, 0, offset == 0)

            def second(offset=offset, chip=chip):
                if work is not None:
                    work(chip, 1, offset == 0)

            jobs += [first, second]
        return jobs

    for d in range(1, reach + 1):
        jobs = jobs_at(d - 1)
        for way, half in PAIRS:
            if not travels(way, half, d, reach):
                continue
            owner = at(-d if way == RIGHT else d, core)
            piece = out_ref.at[owner, :, cols[half]]
            remote(
                piece, piece, ring_send.at[way, d - 1, half], ring_recv.at[way, d - 1, half], mate
            ).wait_recv()
            if travels(way, half, d + 1, reach):
                forward(piece, owner, way, half, d)
            copy = remote(
                piece, piece, mate_send.at[way, d, half], mate_recv.at[way, d, half], mate
            )
            copy.start()
            started.append(copy)
            if jobs:
                jobs.pop(0)()
        for job in jobs:
            job()
    for job in jobs_at(reach):
        job()
    for copy in started:
        copy.wait_send()


def pick_kernel(n, x_ref, place_ref, out_ref, held, chosen, *semaphores):
    count = place_ref.shape[1]
    rows, width = x_ref.shape
    depth = out_ref.shape[0]

    def work(chip, half, start):
        if half == 0:
            places = lax.broadcasted_iota(jnp.int32, (depth, 2 * rows), 0).astype(jnp.float32)
            marks = jnp.zeros((depth, 2 * rows), jnp.float32)
            table = place_ref[chip]
            for e in range(count):
                marks = jnp.where(places == table[e : e + 1], 1.0, marks)
            chosen[...] = marks.astype(jnp.bfloat16)
        steps = width // 2 // COLUMNS_STEP

        @pl.loop(half * steps, (half + 1) * steps)
        def _(c):
            part = pl.ds(pl.multiple_of(c * COLUMNS_STEP, COLUMNS_STEP), COLUMNS_STEP)
            block = held[pl.ds(chip * 2, 2), :, part].reshape(2 * rows, COLUMNS_STEP)
            picked = jnp.dot(chosen[...], block, preferred_element_type=jnp.float32)
            picked = picked.astype(jnp.bfloat16)
            out_ref[:, part] = picked if start else out_ref[:, part] + picked

    gather_kernel(n, x_ref, held, *semaphores, work=work)


def ring_pick(x, places, depth, n, collective_id):
    reach = n // 4
    rows, width = x.shape
    return pl.pallas_call(
        functools.partial(pick_kernel, n),
        out_shape=jax.ShapeDtypeStruct((depth, width), x.dtype),
        in_specs=[VMEM] * 2,
        out_specs=VMEM,
        scratch_shapes=[
            pltpu.VMEM((n, rows, width), x.dtype),
            pltpu.VMEM((depth, 2 * rows), x.dtype),
            pltpu.SemaphoreType.DMA((2, reach, 2)),
            pltpu.SemaphoreType.DMA((2, reach, 2)),
            pltpu.SemaphoreType.DMA((2, reach + 1, 2)),
            pltpu.SemaphoreType.DMA((2, reach + 1, 2)),
        ],
        compiler_params=pltpu.CompilerParams(collective_id=collective_id, has_side_effects=True),
        name=f"pick{collective_id}",
    )(x, places)


def ring_gather(x, n, collective_id):
    reach = n // 4
    return pl.pallas_call(
        functools.partial(gather_kernel, n),
        out_shape=jax.ShapeDtypeStruct((n,) + x.shape, x.dtype),
        in_specs=[VMEM],
        out_specs=VMEM,
        scratch_shapes=[
            pltpu.SemaphoreType.DMA((2, reach, 2)),
            pltpu.SemaphoreType.DMA((2, reach, 2)),
            pltpu.SemaphoreType.DMA((2, reach + 1, 2)),
            pltpu.SemaphoreType.DMA((2, reach + 1, 2)),
        ],
        compiler_params=pltpu.CompilerParams(collective_id=collective_id, has_side_effects=True),
        name=f"gather{collective_id}",
    )(x)


def scatter_kernel(n, finish, left, extras, lhs_ref, rhs_ref, *refs):
    extra_refs, refs = refs[:extras], refs[extras:]
    outs, scratch = refs[:-8], refs[-8:]
    made, from_mate, outgoing, incoming, ring_send, ring_recv, mate_send, mate_recv = scratch
    m, reach = n // 2, n // 4
    me, core, at = ring(m)
    mate = at(0, 1 - core)
    neighbour = (at(1, core), at(-1, core))
    rows, width = made.shape[2:]
    half_width = width // 2
    cols = [pl.ds(h * half_width, half_width) for h in range(2)]
    greet((neighbour[0], neighbour[1], mate))
    started = []
    offsets = [reach]
    for d in range(reach - 1, 0, -1):
        offsets += [d, -d]
    offsets.append(0)
    mate_copies = {}

    def make(offset):
        k = offsets.index(offset)
        lhs = left(lhs_ref[at(offset, 0) // 2], rhs_ref.shape[0])

        @pl.loop(0, width // COLUMNS_STEP)
        def _(c):
            part = pl.ds(pl.multiple_of(c * COLUMNS_STEP, COLUMNS_STEP), COLUMNS_STEP)
            product = jnp.dot(lhs, rhs_ref[:, part], preferred_element_type=jnp.float32)
            product = product.astype(jnp.bfloat16)
            made[k, 0, :, part] = product[:rows]
            made[k, 1, :, part] = product[rows:]

        copy = remote(
            made.at[k, 1 - core], from_mate.at[k], mate_send.at[k], mate_recv.at[k], mate
        )
        copy.start()
        started.append(copy)
        mate_copies[k] = copy

    def make_level(d):
        for offset in offsets:
            if abs(offset) == d:
                make(offset)

    arrived = set()

    def chip_sum(offset, half):
        k = offsets.index(offset)
        if k not in arrived:
            mate_copies[k].wait_recv()
            arrived.add(k)
        mine = made[k, core, :, cols[half]].astype(jnp.float32)
        return mine + from_mate[k, :, cols[half]].astype(jnp.float32)

    def received(way, half, d):
        piece = incoming.at[way, d, half]
        remote(
            piece, piece, ring_send.at[way, d, half], ring_recv.at[way, d, half], mate
        ).wait_recv()
        return incoming[way, d, half].astype(jnp.float32)

    make_level(reach)
    for d in range(reach, 0, -1):
        make_level(d - 1)
        for way, half in ((RIGHT, 1), (LEFT, 0), (RIGHT, 0), (LEFT, 1)):
            if not travels(way, half, d, reach):
                continue
            offset = d if (way == RIGHT or d == reach) else -d
            total = chip_sum(offset, half)
            if travels(way, half, d + 1, reach):
                total = total + received(way, half, d)
            outgoing[way, d - 1, half] = total.astype(jnp.bfloat16)
            copy = remote(
                outgoing.at[way, d - 1, half],
                incoming.at[way, d - 1, half],
                ring_send.at[way, d - 1, half],
                ring_recv.at[way, d - 1, half],
                neighbour[way],
            )
            copy.start()
            started.append(copy)
    totals = [
        chip_sum(0, half) + received(RIGHT, half, 0) + received(LEFT, half, 0) for half in range(2)
    ]
    finish(totals, cols, extra_refs, outs)
    for copy in started:
        copy.wait_send()


def finish_plain(totals, cols, extra_refs, outs):
    for half in range(2):
        outs[0][:, cols[half]] = totals[half].astype(jnp.bfloat16)


def finish_normed(totals, cols, extra_refs, outs):
    residual_ref, gain_ref = extra_refs
    hidden_ref, normed_ref = outs
    squares = 0.0
    for half in range(2):
        hidden = totals[half] + residual_ref[:, cols[half]].astype(jnp.float32)
        hidden = hidden.astype(jnp.bfloat16)
        hidden_ref[:, cols[half]] = hidden
        wide = hidden.astype(jnp.float32)
        squares = squares + jnp.sum(wide * wide, axis=-1, keepdims=True)
    scale = lax.rsqrt(squares / hidden_ref.shape[1] + epsilon)
    for half in range(2):
        wide = hidden_ref[:, cols[half]].astype(jnp.float32)
        normed_ref[:, cols[half]] = (wide * scale * gain_ref[:, cols[half]]).astype(jnp.bfloat16)


def as_it_is(lhs, depth):
    return lhs


def spread(lhs, depth):
    count = lhs.shape[1] // 2
    places = lax.broadcasted_iota(jnp.int32, (lhs.shape[0], depth), 1).astype(jnp.float32)
    total = jnp.zeros((lhs.shape[0], depth), jnp.float32)
    for e in range(count):
        total = jnp.where(
            places == lhs[:, e : e + 1], lhs[:, count + e : count + e + 1], total
        )
    return total.astype(jnp.bfloat16)


def ring_scatter(
    lhs, rhs, n, collective_id, left=as_it_is, finish=finish_plain, extras=(), outputs=1
):
    m, reach = n // 2, n // 4
    rows, width = lhs.shape[1] // 2, rhs.shape[1]
    piece = (2, reach, 2, rows, width // 2)
    return pl.pallas_call(
        functools.partial(scatter_kernel, n, finish, left, len(extras)),
        out_shape=[jax.ShapeDtypeStruct((rows, width), jnp.bfloat16)] * outputs,
        in_specs=[VMEM] * (2 + len(extras)),
        out_specs=[VMEM] * outputs,
        scratch_shapes=[
            pltpu.VMEM((m, 2, rows, width), jnp.bfloat16),
            pltpu.VMEM((m, rows, width), jnp.bfloat16),
            pltpu.VMEM(piece, jnp.bfloat16),
            pltpu.VMEM(piece, jnp.bfloat16),
            pltpu.SemaphoreType.DMA((2, reach, 2)),
            pltpu.SemaphoreType.DMA((2, reach, 2)),
            pltpu.SemaphoreType.DMA((m,)),
            pltpu.SemaphoreType.DMA((m,)),
        ],
        compiler_params=pltpu.CompilerParams(collective_id=collective_id, has_side_effects=True),
        name=f"scatter{collective_id}",
    )(lhs, rhs, *extras)


def attend_kernel(n, key_count, q_ref, fresh_ref, cached_ref, out_ref, stage, send, recv):
    me = lax.axis_index("ctx")
    rows = q_ref.shape[0]
    per = QUERY_HEADS // n
    group = HEADS_STEP // per
    steps = n // group
    scale = HEAD_SIZE ** (-0.5)
    greet([(me + j) % n for j in range(1, n)])

    def heads_of(u):
        pair = u * HEADS_STEP // (QUERY_HEADS // KEY_VALUE_HEADS)
        lanes = pl.ds(pl.multiple_of(pair * HEAD_SIZE, HEAD_SIZE), HEAD_SIZE)
        keys = cached_ref[:, :key_count, lanes].reshape(-1, HEAD_SIZE)
        values = cached_ref[:, key_count : 2 * key_count, lanes].reshape(-1, HEAD_SIZE)
        fresh_key = fresh_ref[0, :, lanes].astype(jnp.float32)
        fresh_value = fresh_ref[1, :, lanes].astype(jnp.float32)
        width = HEADS_STEP * HEAD_SIZE
        block = q_ref[:, pl.ds(pl.multiple_of(u * width, width), width)]
        heads = [block[:, h * HEAD_SIZE : (h + 1) * HEAD_SIZE] for h in range(HEADS_STEP)]
        scores = (
            lax.dot_general(
                jnp.concatenate(heads, axis=0),
                keys,
                (((1,), (1,)), ((), ())),
                preferred_element_type=jnp.float32,
            )
            * scale
        )
        own = jnp.concatenate(
            [jnp.sum(q.astype(jnp.float32) * fresh_key, axis=-1, keepdims=True) for q in heads],
            axis=0,
        )
        own = own * scale
        peak = jnp.maximum(own, jnp.max(scores, axis=-1, keepdims=True))
        weights = jnp.exp(scores - peak)
        own = jnp.exp(own - peak)
        totals = jnp.sum(weights, axis=-1, keepdims=True) + own
        mixed = jnp.dot(weights.astype(jnp.bfloat16), values, preferred_element_type=jnp.float32)
        for h in range(HEADS_STEP):
            part = slice(h * rows, (h + 1) * rows)
            result = (mixed[part] + own[part] * fresh_value) / totals[part]
            column = (h % per) * HEAD_SIZE
            stage[u * group + h // per, :, column : column + HEAD_SIZE] = result.astype(
                jnp.bfloat16
            )

    def copy_to(other):
        return remote(stage.at[other], out_ref.at[me], send.at[other], recv.at[me], other)

    @pl.loop(0, steps - 1)
    def _(s):
        u = (me // group + 1 + s) % steps
        heads_of(u)
        for j in range(group):
            copy_to(u * group + j).start()

    heads_of(me // group)
    near = [me // group * group + (me % group + j) % group for j in range(1, group)]
    for other in near:
        copy_to(other).start()
    out_ref[me] = stage[me]
    for j in range(1, n):
        source = (me + n - j) % n
        piece = out_ref.at[source]
        remote(piece, piece, send.at[source], recv.at[source], source).wait_recv()
    for j in range(1, n):
        copy_to((me + j) % n).wait_send()


def attend(queries, fresh_key_value, gathered, key_count, n, collective_id):
    rows = queries.shape[0]
    shape = (n, rows, QUERY_HEADS // n * HEAD_SIZE)
    return pl.pallas_call(
        functools.partial(attend_kernel, n, key_count),
        out_shape=jax.ShapeDtypeStruct(shape, jnp.bfloat16),
        in_specs=[VMEM] * 3,
        out_specs=VMEM,
        scratch_shapes=[
            pltpu.VMEM(shape, jnp.bfloat16),
            pltpu.SemaphoreType.DMA((n,)),
            pltpu.SemaphoreType.DMA((n,)),
        ],
        compiler_params=pltpu.CompilerParams(collective_id=collective_id, has_side_effects=True),
        name="attend",
    )(queries, fresh_key_value, gathered)


def local(
    n,
    queries,
    fresh_key_value,
    cache_key_value,
    residual,
    norm_gain,
    out_proj,
    w_gate_up,
    w_down,
    route_ids,
    route_weights,
    placement,
):
    rows = queries.shape[0]
    expert_count = placement.shape[0]
    local_count = w_gate_up.shape[0]
    key_count = cache_key_value.shape[1]
    kv_width = cache_key_value.shape[2]
    capacity = n * max(2, 3 * rows * TOPK // (2 * expert_count))

    gate_share = route_weights / jnp.sum(route_weights, axis=-1, keepdims=True)
    slots = jnp.sum(
        jnp.where(route_ids[..., None] == jnp.arange(expert_count), placement, 0), axis=-1
    )
    slot_lanes = -(-expert_count // 128) * 128
    shares = jnp.sum(
        jnp.where(slots[..., None] == jnp.arange(slot_lanes), gate_share[..., None], 0.0), axis=1
    ).astype(jnp.bfloat16)
    share_rows = rows * slot_lanes // kv_width
    padded = -(-share_rows // 16) * 16
    packed = jnp.concatenate(
        [
            cache_key_value.reshape(2 * key_count, kv_width),
            jnp.pad(shares.reshape(share_rows, kv_width), ((0, padded - share_rows), (0, 0))),
        ],
        axis=0,
    )
    gathered = ring_gather(packed, n, 0)

    mine = lax.axis_index("ctx") * local_count
    all_shares = gathered[:, 2 * key_count : 2 * key_count + share_rows].reshape(
        n * rows, slot_lanes
    )
    my_shares = lax.dynamic_slice(all_shares, (0, mine), (n * rows, local_count)).T
    named = my_shares > 0
    ranks = jnp.cumsum(named.astype(jnp.int32), axis=1) - 1
    starts = jnp.arange(local_count)[:, None] * capacity
    places = jnp.where(named, ranks + starts, -1).astype(jnp.float32)
    table = places.reshape(local_count, n // 2, 2 * rows).transpose(1, 0, 2)
    listed = jnp.concatenate([places, my_shares.astype(jnp.float32)], axis=0)
    listed = listed.reshape(2 * local_count, n // 2, 2 * rows).transpose(1, 2, 0)

    attention = attend(queries, fresh_key_value, gathered, key_count, n, 1)
    hidden, normed = ring_scatter(
        attention.reshape(n // 2, 2 * rows, -1),
        out_proj,
        n,
        2,
        as_it_is,
        finish_normed,
        (residual, norm_gain.reshape(1, D)),
        2,
    )
    inputs = ring_pick(normed, table, local_count * capacity, n, 3)
    inputs = inputs.reshape(local_count, capacity, D)
    both = jnp.einsum("emd,edf->emf", inputs, w_gate_up, preferred_element_type=jnp.float32)
    active = (jax.nn.silu(both[..., :FF]) * both[..., FF:]).astype(jnp.bfloat16)
    produced = jnp.einsum(
        "emf,efd->emd", active, w_down, preferred_element_type=jnp.float32
    ).astype(jnp.bfloat16)
    (expert_out,) = ring_scatter(
        listed, produced.reshape(local_count * capacity, D), n, 4, spread
    )
    return (hidden, expert_out)


def solution(mesh):
    in_specs = (
        P(("groups", "ctx"), None),
        P(None, ("groups", "ctx"), None),
        P(None, ("groups", "ctx"), None),
        P(("groups", "ctx"), None),
        P(),
        P("ctx", None),
        P("ctx", None, None),
        P("ctx", None, None),
        P(("groups", "ctx"), None),
        P(("groups", "ctx"), None),
        P(),
    )
    out_specs = (P(("groups", "ctx"), None), P(("groups", "ctx"), None))
    return jax.shard_map(
        functools.partial(local, mesh.shape["ctx"]),
        mesh=mesh,
        in_specs=in_specs,
        out_specs=out_specs,
        check_vma=False,
    )
```

```python
import functools

import jax
import jax.numpy as jnp
from jax import lax
from jax.experimental import pallas as pl
from jax.experimental.pallas import tpu as pltpu
from jax.sharding import PartitionSpec as P

D = 2048
QUERY_HEADS = 32
KEY_VALUE_HEADS = 4
HEAD_SIZE = 128
FF = 768
TOPK = 8
HEADS_STEP = 4
COLUMNS_STEP = 512

epsilon = 1e-06

VMEM = pl.BlockSpec(memory_space=pltpu.VMEM)
RIGHT, LEFT = 0, 1


def chip_at(q, m):
    return jnp.where(q < m // 2, 2 * q, 2 * (m - 1 - q) + 1)


def place_of(chip, m):
    return jnp.where(chip % 2 == 0, chip // 2, m - 1 - chip // 2)


def ring(m):
    me = lax.axis_index("ctx")
    core, p = me % 2, place_of(me // 2, m)

    def at(offset, c):
        return chip_at((p + offset + m) % m, m) * 2 + c

    return me, core, at


def greet(others):
    barrier = pltpu.get_barrier_semaphore()
    for other in others:
        pl.semaphore_signal(
            barrier, inc=1, device_id={"ctx": other}, device_id_type=pl.DeviceIdType.MESH
        )
    pl.semaphore_wait(barrier, len(others))


def remote(src, dst, send, recv, other):
    return pltpu.make_async_remote_copy(
        src_ref=src,
        dst_ref=dst,
        send_sem=send,
        recv_sem=recv,
        device_id={"ctx": other},
        device_id_type=pl.DeviceIdType.MESH,
    )


def travels(way, half, d, reach):
    return d < reach or (d == reach and half == way)


PAIRS = ((RIGHT, 0), (LEFT, 1), (RIGHT, 1), (LEFT, 0))


def gather_kernel(n, x_ref, out_ref, ring_send, ring_recv, mate_send, mate_recv, work=None, met=False):
    m, reach = n // 2, n // 4
    me, core, at = ring(m)
    mate = at(0, 1 - core)
    neighbour = (at(1, core), at(-1, core))
    half_width = x_ref.shape[1] // 2
    cols = [pl.ds(h * half_width, half_width) for h in range(2)]
    if not met:
        greet((neighbour[0], neighbour[1], mate))
    started = []

    def forward(src, owner, way, half, d):
        copy = remote(
            src,
            out_ref.at[owner, :, cols[half]],
            ring_send.at[way, d, half],
            ring_recv.at[way, d, half],
            neighbour[way],
        )
        copy.start()
        started.append(copy)

    for way, half in PAIRS:
        forward(x_ref.at[:, cols[half]], me, way, half, 0)
    copy = remote(x_ref, out_ref.at[me], mate_send.at[0, 0, 0], mate_recv.at[0, 0, 0], mate)
    copy.start()
    started.append(copy)
    out_ref[me] = x_ref[...]
    def wait_mate(offset):
        if offset == 0:
            theirs = out_ref.at[mate]
            remote(theirs, theirs, mate_send.at[0, 0, 0], mate_recv.at[0, 0, 0], mate).wait_recv()
            return
        d = abs(offset)
        for way, half in PAIRS:
            if travels(way, half, d, reach) and (d == reach or (way == RIGHT) == (offset < 0)):
                piece = out_ref.at[at(offset, 1 - core), :, cols[half]]
                remote(
                    piece, piece, mate_send.at[way, d, half], mate_recv.at[way, d, half], mate
                ).wait_recv()

    def offsets_at(d):
        return [d] if d in (0, reach) else [-d, d]

    def jobs_at(d):
        jobs = []
        for offset in offsets_at(d):
            chip = at(offset, 0) // 2

            def first(offset=offset, chip=chip):
                wait_mate(offset)
                if work is not None:
                    work(chip, 0, offset == 0)

            def second(offset=offset, chip=chip):
                if work is not None:
                    work(chip, 1, offset == 0)

            jobs += [first, second]
        return jobs

    for d in range(1, reach + 1):
        jobs = jobs_at(d - 1)
        for way, half in PAIRS:
            if not travels(way, half, d, reach):
                continue
            owner = at(-d if way == RIGHT else d, core)
            piece = out_ref.at[owner, :, cols[half]]
            remote(
                piece, piece, ring_send.at[way, d - 1, half], ring_recv.at[way, d - 1, half], mate
            ).wait_recv()
            if travels(way, half, d + 1, reach):
                forward(piece, owner, way, half, d)
            copy = remote(
                piece, piece, mate_send.at[way, d, half], mate_recv.at[way, d, half], mate
            )
            copy.start()
            started.append(copy)
            if jobs:
                jobs.pop(0)()
        for job in jobs:
            job()
    for job in jobs_at(reach):
        job()
    for copy in started:
        copy.wait_send()


def pick_kernel(n, x_ref, place_ref, out_ref, held, chosen, *semaphores):
    count = place_ref.shape[1]
    rows, width = x_ref.shape
    depth = out_ref.shape[0]

    def work(chip, half, start):
        if half == 0:
            places = lax.broadcasted_iota(jnp.int32, (depth, 2 * rows), 0).astype(jnp.float32)
            marks = jnp.zeros((depth, 2 * rows), jnp.float32)
            table = place_ref[chip]
            for e in range(count):
                marks = jnp.where(places == table[e : e + 1], 1.0, marks)
            chosen[...] = marks.astype(jnp.bfloat16)
        steps = width // 2 // COLUMNS_STEP

        @pl.loop(half * steps, (half + 1) * steps)
        def _(c):
            part = pl.ds(pl.multiple_of(c * COLUMNS_STEP, COLUMNS_STEP), COLUMNS_STEP)
            block = held[pl.ds(chip * 2, 2), :, part].reshape(2 * rows, COLUMNS_STEP)
            picked = jnp.dot(chosen[...], block, preferred_element_type=jnp.float32)
            picked = picked.astype(jnp.bfloat16)
            out_ref[:, part] = picked if start else out_ref[:, part] + picked

    gather_kernel(n, x_ref, held, *semaphores, work=work, met=True)


def ring_gather(x, n, collective_id):
    reach = n // 4
    return pl.pallas_call(
        functools.partial(gather_kernel, n),
        out_shape=jax.ShapeDtypeStruct((n,) + x.shape, x.dtype),
        in_specs=[VMEM],
        out_specs=VMEM,
        scratch_shapes=[
            pltpu.SemaphoreType.DMA((2, reach, 2)),
            pltpu.SemaphoreType.DMA((2, reach, 2)),
            pltpu.SemaphoreType.DMA((2, reach + 1, 2)),
            pltpu.SemaphoreType.DMA((2, reach + 1, 2)),
        ],
        compiler_params=pltpu.CompilerParams(collective_id=collective_id, has_side_effects=True),
        name=f"gather{collective_id}",
    )(x)


def scatter_kernel(n, finish, left, extras, lhs_ref, rhs_ref, *refs):
    extra_refs, refs = refs[:extras], refs[extras:]
    outs, scratch = refs[:-8], refs[-8:]
    made, from_mate, outgoing, incoming, ring_send, ring_recv, mate_send, mate_recv = scratch
    m, reach = n // 2, n // 4
    me, core, at = ring(m)
    mate = at(0, 1 - core)
    neighbour = (at(1, core), at(-1, core))
    rows, width = made.shape[2:]
    half_width = width // 2
    cols = [pl.ds(h * half_width, half_width) for h in range(2)]
    greet((neighbour[0], neighbour[1], mate))
    started = []
    offsets = [reach]
    for d in range(reach - 1, 0, -1):
        offsets += [d, -d]
    offsets.append(0)
    mate_copies = {}

    def make(offset):
        k = offsets.index(offset)
        lhs = left(lhs_ref[at(offset, 0) // 2], rhs_ref.shape[0])

        @pl.loop(0, width // COLUMNS_STEP)
        def _(c):
            part = pl.ds(pl.multiple_of(c * COLUMNS_STEP, COLUMNS_STEP), COLUMNS_STEP)
            product = jnp.dot(lhs, rhs_ref[:, part], preferred_element_type=jnp.float32)
            product = product.astype(jnp.bfloat16)
            made[k, 0, :, part] = product[:rows]
            made[k, 1, :, part] = product[rows:]

        copy = remote(
            made.at[k, 1 - core], from_mate.at[k], mate_send.at[k], mate_recv.at[k], mate
        )
        copy.start()
        started.append(copy)
        mate_copies[k] = copy

    def make_level(d):
        for offset in offsets:
            if abs(offset) == d:
                make(offset)

    arrived = set()

    def chip_sum(offset, half):
        k = offsets.index(offset)
        if k not in arrived:
            mate_copies[k].wait_recv()
            arrived.add(k)
        mine = made[k, core, :, cols[half]].astype(jnp.float32)
        return mine + from_mate[k, :, cols[half]].astype(jnp.float32)

    def received(way, half, d):
        piece = incoming.at[way, d, half]
        remote(
            piece, piece, ring_send.at[way, d, half], ring_recv.at[way, d, half], mate
        ).wait_recv()
        return incoming[way, d, half].astype(jnp.float32)

    make_level(reach)
    for d in range(reach, 0, -1):
        make_level(d - 1)
        for way, half in ((RIGHT, 1), (LEFT, 0), (RIGHT, 0), (LEFT, 1)):
            if not travels(way, half, d, reach):
                continue
            offset = d if (way == RIGHT or d == reach) else -d
            total = chip_sum(offset, half)
            if travels(way, half, d + 1, reach):
                total = total + received(way, half, d)
            outgoing[way, d - 1, half] = total.astype(jnp.bfloat16)
            copy = remote(
                outgoing.at[way, d - 1, half],
                incoming.at[way, d - 1, half],
                ring_send.at[way, d - 1, half],
                ring_recv.at[way, d - 1, half],
                neighbour[way],
            )
            copy.start()
            started.append(copy)
    totals = [
        chip_sum(0, half) + received(RIGHT, half, 0) + received(LEFT, half, 0) for half in range(2)
    ]
    finish(totals, cols, extra_refs, outs)
    for copy in started:
        copy.wait_send()


def finish_plain(totals, cols, extra_refs, outs):
    for half in range(2):
        outs[0][:, cols[half]] = totals[half].astype(jnp.bfloat16)


def finish_normed(totals, cols, extra_refs, outs):
    residual_ref, gain_ref = extra_refs
    hidden_ref, normed_ref = outs
    squares = 0.0
    for half in range(2):
        hidden = totals[half] + residual_ref[:, cols[half]].astype(jnp.float32)
        hidden = hidden.astype(jnp.bfloat16)
        hidden_ref[:, cols[half]] = hidden
        wide = hidden.astype(jnp.float32)
        squares = squares + jnp.sum(wide * wide, axis=-1, keepdims=True)
    scale = lax.rsqrt(squares / hidden_ref.shape[1] + epsilon)
    for half in range(2):
        wide = hidden_ref[:, cols[half]].astype(jnp.float32)
        normed_ref[:, cols[half]] = (wide * scale * gain_ref[:, cols[half]]).astype(jnp.bfloat16)


def as_it_is(lhs, depth):
    return lhs


def spread(lhs, depth):
    count = lhs.shape[1] // 2
    places = lax.broadcasted_iota(jnp.int32, (lhs.shape[0], depth), 1).astype(jnp.float32)
    total = jnp.zeros((lhs.shape[0], depth), jnp.float32)
    for e in range(count):
        total = jnp.where(
            places == lhs[:, e : e + 1], lhs[:, count + e : count + e + 1], total
        )
    return total.astype(jnp.bfloat16)


def ring_scatter(
    lhs, rhs, n, collective_id, left=as_it_is, finish=finish_plain, extras=(), outputs=1
):
    m, reach = n // 2, n // 4
    rows, width = lhs.shape[1] // 2, rhs.shape[1]
    piece = (2, reach, 2, rows, width // 2)
    return pl.pallas_call(
        functools.partial(scatter_kernel, n, finish, left, len(extras)),
        out_shape=[jax.ShapeDtypeStruct((rows, width), jnp.bfloat16)] * outputs,
        in_specs=[VMEM] * (2 + len(extras)),
        out_specs=[VMEM] * outputs,
        scratch_shapes=[
            pltpu.VMEM((m, 2, rows, width), jnp.bfloat16),
            pltpu.VMEM((m, rows, width), jnp.bfloat16),
            pltpu.VMEM(piece, jnp.bfloat16),
            pltpu.VMEM(piece, jnp.bfloat16),
            pltpu.SemaphoreType.DMA((2, reach, 2)),
            pltpu.SemaphoreType.DMA((2, reach, 2)),
            pltpu.SemaphoreType.DMA((m,)),
            pltpu.SemaphoreType.DMA((m,)),
        ],
        compiler_params=pltpu.CompilerParams(collective_id=collective_id, has_side_effects=True),
        name=f"scatter{collective_id}",
    )(lhs, rhs, *extras)


def scatter_pick_kernel(
    n, lhs_ref, rhs_ref, residual_ref, gain_ref, place_ref, hidden_ref, out_ref, *scratch
):
    normed, scratch = scratch[0], scratch[1:]
    scatter_kernel(
        n,
        finish_normed,
        as_it_is,
        2,
        lhs_ref,
        rhs_ref,
        residual_ref,
        gain_ref,
        hidden_ref,
        normed,
        *scratch[:8],
    )
    pick_kernel(n, normed, place_ref, out_ref, *scratch[8:])


def scatter_pick(lhs, rhs, residual, gain, places, depth, n, collective_id):
    m, reach = n // 2, n // 4
    rows, width = residual.shape
    piece = (2, reach, 2, rows, width // 2)
    return pl.pallas_call(
        functools.partial(scatter_pick_kernel, n),
        out_shape=[
            jax.ShapeDtypeStruct((rows, width), jnp.bfloat16),
            jax.ShapeDtypeStruct((depth, width), jnp.bfloat16),
        ],
        in_specs=[VMEM] * 5,
        out_specs=[VMEM] * 2,
        scratch_shapes=[
            pltpu.VMEM((rows, width), jnp.bfloat16),
            pltpu.VMEM((m, 2, rows, width), jnp.bfloat16),
            pltpu.VMEM((m, rows, width), jnp.bfloat16),
            pltpu.VMEM(piece, jnp.bfloat16),
            pltpu.VMEM(piece, jnp.bfloat16),
            pltpu.SemaphoreType.DMA((2, reach, 2)),
            pltpu.SemaphoreType.DMA((2, reach, 2)),
            pltpu.SemaphoreType.DMA((m,)),
            pltpu.SemaphoreType.DMA((m,)),
            pltpu.VMEM((n, rows, width), jnp.bfloat16),
            pltpu.VMEM((depth, 2 * rows), jnp.bfloat16),
            pltpu.SemaphoreType.DMA((2, reach, 2)),
            pltpu.SemaphoreType.DMA((2, reach, 2)),
            pltpu.SemaphoreType.DMA((2, reach + 1, 2)),
            pltpu.SemaphoreType.DMA((2, reach + 1, 2)),
        ],
        compiler_params=pltpu.CompilerParams(collective_id=collective_id, has_side_effects=True),
        name=f"scatter_pick{collective_id}",
    )(lhs, rhs, residual, gain, places)


def attend_kernel(n, key_count, q_ref, fresh_ref, cached_ref, out_ref, stage, send, recv):
    me = lax.axis_index("ctx")
    rows = q_ref.shape[0]
    per = QUERY_HEADS // n
    group = HEADS_STEP // per
    steps = n // group
    scale = HEAD_SIZE ** (-0.5)
    greet([(me + j) % n for j in range(1, n)])

    def heads_of(u):
        pair = u * HEADS_STEP // (QUERY_HEADS // KEY_VALUE_HEADS)
        lanes = pl.ds(pl.multiple_of(pair * HEAD_SIZE, HEAD_SIZE), HEAD_SIZE)
        keys = cached_ref[:, :key_count, lanes].reshape(-1, HEAD_SIZE)
        values = cached_ref[:, key_count : 2 * key_count, lanes].reshape(-1, HEAD_SIZE)
        fresh_key = fresh_ref[0, :, lanes].astype(jnp.float32)
        fresh_value = fresh_ref[1, :, lanes].astype(jnp.float32)
        width = HEADS_STEP * HEAD_SIZE
        block = q_ref[:, pl.ds(pl.multiple_of(u * width, width), width)]
        heads = [block[:, h * HEAD_SIZE : (h + 1) * HEAD_SIZE] for h in range(HEADS_STEP)]
        scores = (
            lax.dot_general(
                jnp.concatenate(heads, axis=0),
                keys,
                (((1,), (1,)), ((), ())),
                preferred_element_type=jnp.float32,
            )
            * scale
        )
        own = jnp.concatenate(
            [jnp.sum(q.astype(jnp.float32) * fresh_key, axis=-1, keepdims=True) for q in heads],
            axis=0,
        )
        own = own * scale
        peak = jnp.maximum(own, jnp.max(scores, axis=-1, keepdims=True))
        weights = jnp.exp(scores - peak)
        own = jnp.exp(own - peak)
        totals = jnp.sum(weights, axis=-1, keepdims=True) + own
        mixed = jnp.dot(weights.astype(jnp.bfloat16), values, preferred_element_type=jnp.float32)
        for h in range(HEADS_STEP):
            part = slice(h * rows, (h + 1) * rows)
            result = (mixed[part] + own[part] * fresh_value) / totals[part]
            column = (h % per) * HEAD_SIZE
            stage[u * group + h // per, :, column : column + HEAD_SIZE] = result.astype(
                jnp.bfloat16
            )

    def copy_to(other):
        return remote(stage.at[other], out_ref.at[me], send.at[other], recv.at[me], other)

    @pl.loop(0, steps - 1)
    def _(s):
        u = (me // group + 1 + s) % steps
        heads_of(u)
        for j in range(group):
            copy_to(u * group + j).start()

    heads_of(me // group)
    near = [me // group * group + (me % group + j) % group for j in range(1, group)]
    for other in near:
        copy_to(other).start()
    out_ref[me] = stage[me]
    for j in range(1, n):
        source = (me + n - j) % n
        piece = out_ref.at[source]
        remote(piece, piece, send.at[source], recv.at[source], source).wait_recv()
    for j in range(1, n):
        copy_to((me + j) % n).wait_send()


def attend(queries, fresh_key_value, gathered, key_count, n, collective_id):
    rows = queries.shape[0]
    shape = (n, rows, QUERY_HEADS // n * HEAD_SIZE)
    return pl.pallas_call(
        functools.partial(attend_kernel, n, key_count),
        out_shape=jax.ShapeDtypeStruct(shape, jnp.bfloat16),
        in_specs=[VMEM] * 3,
        out_specs=VMEM,
        scratch_shapes=[
            pltpu.VMEM(shape, jnp.bfloat16),
            pltpu.SemaphoreType.DMA((n,)),
            pltpu.SemaphoreType.DMA((n,)),
        ],
        compiler_params=pltpu.CompilerParams(collective_id=collective_id, has_side_effects=True),
        name="attend",
    )(queries, fresh_key_value, gathered)


def local(
    n,
    queries,
    fresh_key_value,
    cache_key_value,
    residual,
    norm_gain,
    out_proj,
    w_gate_up,
    w_down,
    route_ids,
    route_weights,
    placement,
):
    rows = queries.shape[0]
    expert_count = placement.shape[0]
    local_count = w_gate_up.shape[0]
    key_count = cache_key_value.shape[1]
    kv_width = cache_key_value.shape[2]
    capacity = n * max(2, 3 * rows * TOPK // (2 * expert_count))

    gate_share = route_weights / jnp.sum(route_weights, axis=-1, keepdims=True)
    slots = jnp.sum(
        jnp.where(route_ids[..., None] == jnp.arange(expert_count), placement, 0), axis=-1
    )
    slot_lanes = expert_count
    shares = jnp.sum(
        jnp.where(slots[..., None] == jnp.arange(slot_lanes), gate_share[..., None], 0.0), axis=1
    ).astype(jnp.bfloat16)
    share_rows = rows * slot_lanes // kv_width
    padded = -(-share_rows // 16) * 16
    packed = jnp.concatenate(
        [
            cache_key_value.reshape(2 * key_count, kv_width),
            jnp.pad(shares.reshape(share_rows, kv_width), ((0, padded - share_rows), (0, 0))),
        ],
        axis=0,
    )
    gathered = ring_gather(packed, n, 0)

    mine = lax.axis_index("ctx") * local_count
    all_shares = gathered[:, 2 * key_count : 2 * key_count + share_rows].reshape(
        n * rows, slot_lanes
    )
    my_shares = lax.dynamic_slice(all_shares, (0, mine), (n * rows, local_count)).T
    named = my_shares > 0
    ranks = jnp.cumsum(named.astype(jnp.int32), axis=1) - 1
    starts = jnp.arange(local_count)[:, None] * capacity
    places = jnp.where(named, ranks + starts, -1).astype(jnp.float32)
    table = places.reshape(local_count, n // 2, 2 * rows).transpose(1, 0, 2)
    listed = jnp.concatenate([places, my_shares.astype(jnp.float32)], axis=0)
    listed = listed.reshape(2 * local_count, n // 2, 2 * rows).transpose(1, 2, 0)

    attention = attend(queries, fresh_key_value, gathered, key_count, n, 1)
    hidden, inputs = scatter_pick(
        attention.reshape(n // 2, 2 * rows, -1),
        out_proj,
        residual,
        norm_gain.reshape(1, D),
        table,
        local_count * capacity,
        n,
        2,
    )
    inputs = inputs.reshape(local_count, capacity, D)
    both = jnp.einsum("emd,edf->emf", inputs, w_gate_up, preferred_element_type=jnp.float32)
    active = (jax.nn.silu(both[..., :FF]) * both[..., FF:]).astype(jnp.bfloat16)
    produced = jnp.einsum(
        "emf,efd->emd", active, w_down, preferred_element_type=jnp.float32
    ).astype(jnp.bfloat16)
    (expert_out,) = ring_scatter(
        listed, produced.reshape(local_count * capacity, D), n, 4, spread
    )
    return (hidden, expert_out)


def solution(mesh):
    in_specs = (
        P(("groups", "ctx"), None),
        P(None, ("groups", "ctx"), None),
        P(None, ("groups", "ctx"), None),
        P(("groups", "ctx"), None),
        P(),
        P("ctx", None),
        P("ctx", None, None),
        P("ctx", None, None),
        P(("groups", "ctx"), None),
        P(("groups", "ctx"), None),
        P(),
    )
    out_specs = (P(("groups", "ctx"), None), P(("groups", "ctx"), None))
    return jax.shard_map(
        functools.partial(local, mesh.shape["ctx"]),
        mesh=mesh,
        in_specs=in_specs,
        out_specs=out_specs,
        check_vma=False,
    )
```
